32 devices in a mesh: seq: 16 (over z, y, core), head: 2 (over x).
Axes of the slice: x: 2, y: 2, z: 4, core: 2. Of those that a mesh axis runs over, the one named last changes fastest.
Arguments:
- query_feats: bfloat16 [8192, 4096], P('seq', 'head'), may hold values from -16 to 16
- key_feats: bfloat16 [8192, 1024], P('seq', 'head'), may hold values from -7 to 7
- value_feats: bfloat16 [8192, 1024], P('seq', 'head'), may hold values from -6 to 6
- span_class: int32 [32], replicated, may hold values from 1 to 16, as said below
- ramp_width: int32 [32], replicated, may hold values from 32 to 128
- doc_lengths: int32 [4], replicated, may hold values from 1 to 4096, 8192 in all
- out_proj: bfloat16 [4096, 4096], P('seq', 'head'), may hold values from -0.5 to 0.5
Outputs:
- mixed: bfloat16 [8192, 4096], P(('seq', 'head'))
The draws below stay inside these ranges and needn't reach their ends.
Inputs may be any that keep to these rules, and one draw needn't show every extreme that they name: `span_class`: some head has a span of 16 tiles.
All inputs are finite; a program needn't handle non-finite values.
Results may differ from the reference program's by a relative error of at most 0.014.
Values may be sent and summed in bfloat16 or wider, within the bound.
No kernel may reach another device: no remote copies, remote signals or barrier semaphores. Data moves between devices by JAX's collectives and lax.ppermute only.
A program may use at most 128 MiB of HBM per device.

```python
import math
import jax
import jax.numpy as jnp
import numpy as np
from jax import lax

D = 4096
H = 32
KVH = 8
HD = 128
TOK_DEV = 512
TILE = 128
MAXBLK = 16
BACK = 4
GROUP_HEADS = 16
TOKENS = 8192
NDOCS = 4
N_SEQ = 16
N_HEAD = 2


def draw_query_feats(key, part):
    result = jnp.clip(1.5 * jax.random.normal(jax.random.fold_in(key, 21), (TOKENS, H * HD), jnp.float32), -6.0, 6.0)
    return result.astype(jnp.bfloat16)


def draw_key_feats(key, part):
    result = jnp.clip(jax.random.normal(jax.random.fold_in(key, 31), (TOKENS, KVH * HD), jnp.float32), -4.0, 4.0)
    return result.astype(jnp.bfloat16)


def draw_span_class(key, part):
    first_draw = jax.random.randint(jax.random.fold_in(key, 41), (H,), 1, MAXBLK + 1)
    second_draw = jax.random.randint(jax.random.fold_in(key, 42), (H,), 1, MAXBLK + 1)
    skewed = jnp.maximum(first_draw * second_draw // MAXBLK, 1)
    longest = jax.random.randint(jax.random.fold_in(key, 43), (), 0, H)
    return jnp.where(jnp.arange(H, dtype=jnp.int32) == longest, MAXBLK, skewed).astype(jnp.int32)


def place_ends(entries, key, least, top_value):
    shape = entries.shape
    spot = [jax.random.randint(jax.random.fold_in(key, axis), (), 0, shape[axis]) for axis in range(len(shape))]
    entries = entries.at[tuple(spot)].set(least)
    longest = shape.index(max(shape))
    spot[longest] = (spot[longest] + 1) % shape[longest]
    return entries.at[tuple(spot)].set(top_value)


def block_scale(rng, extent, pieces, least, high):
    def one(dim, shards_of):
        heights = jax.random.uniform(jax.random.fold_in(jax.random.fold_in(rng, 6), dim), (shards_of,), jnp.float32, least / len(pieces), high / len(pieces))
        return jnp.repeat(jnp.exp(heights), extent[dim] // shards_of).reshape((-1,) + (1,) * (len(extent) - dim - 1))

    gain = one(*pieces[0])
    for cut in pieces[1:]:
        gain = gain * one(*cut)
    return gain


def split_up(number_of, total, most, slope):
    loads = [(1 << 20) // math.isqrt(grade ** slope) + 1 for grade in range(2, number_of + 1)]
    spare, holding = total - most - (number_of - 1), [1] * (number_of - 1)
    while spare > 0:
        free = [i for i in range(number_of - 1) if holding[i] < most]
        whole, budget = sum([loads[i] for i in free]), spare
        for i in free:
            extra = min(most - holding[i], max(1, budget * loads[i] // whole), spare)
            holding[i] = holding[i] + extra
            spare = spare - extra
    return np.array([most] + holding)


def uneven_parts(key, count, total, most, slope):
    if count == 2:
        one = jax.random.randint(key, (), max(1, total - most), min(most, total - 1) + 1)
        return jnp.stack([one, total - one])
    lengths = jnp.asarray(split_up(count, total, most, slope), jnp.int32)
    couples = (count - 1) // 2
    source_of, taker = lengths[1:1 + 2 * couples:2], lengths[2:2 + 2 * couples:2]
    room = jnp.minimum(source_of - 1, most - taker)
    shifted = jax.random.randint(jax.random.fold_in(key, 1), (couples,), 0, 1 << 20) % (room + 1)
    lengths = lengths.at[1:1 + 2 * couples:2].set(source_of - shifted).at[2:2 + 2 * couples:2].set(taker + shifted)
    return lengths[jax.random.permutation(jax.random.fold_in(key, 2), count)]


def scatter_about(key, dims, width, reach, cuts=(), kind=jnp.bfloat16):
    array = jax.random.normal(key, dims, jnp.float32) * width
    if len(cuts) > 0:
        array = block_scale(key, dims, cuts, -0.22, 0.18) * array
    return jnp.clip(array, min=-reach, max=reach).astype(kind)


def setup_inputs(seed: int = 0) -> dict:
    key_of = jax.random.split(jax.random.key(seed), 8)
    query_feats = draw_query_feats(jax.random.fold_in(key_of[7], 71), 0)
    key_feats = draw_key_feats(jax.random.fold_in(key_of[7], 71), 0)
    value_feats = scatter_about(key_of[2], (TOKENS, KVH * HD), 1.0, 6.0, ((0, 16), (1, 2)))
    span_class = draw_span_class(jax.random.fold_in(key_of[7], 71), 0)
    ramp_width = place_ends(jax.random.randint(key_of[4], (H,), TILE // 4, TILE + 1), jax.random.fold_in(key_of[4], 1), TILE // 4, TILE).astype(jnp.int32)
    doc_lengths = uneven_parts(key_of[5], NDOCS, TOKENS, TOKENS // 2, 2).astype(jnp.int32)
    out_proj = scatter_about(key_of[6], (D, H * HD), HD ** -0.5, 0.5, ((0, 16), (1, 2)))
    return dict(query_feats=query_feats, key_feats=key_feats, value_feats=value_feats, span_class=span_class, ramp_width=ramp_width, doc_lengths=doc_lengths, out_proj=out_proj)


very_low = -1e+30

def reference(query_feats, key_feats, value_feats, span_class, ramp_width, doc_lengths, out_proj):
    window = (BACK + 1) * TOK_DEV
    group_width = GROUP_HEADS * HD
    ratio = H // KVH
    starts = jnp.cumsum(doc_lengths) - doc_lengths
    span_end = (span_class * TILE).astype(jnp.float32)
    ramp_float = ramp_width.astype(jnp.float32)
    pad_rows = jnp.zeros((BACK * TOK_DEV, KVH * HD), key_feats.dtype)
    key_pad = jnp.concatenate([pad_rows, key_feats], axis=0)
    value_pad = jnp.concatenate([pad_rows, value_feats], axis=0)

    def one_block(block):
        first = (block * TOK_DEV).astype(jnp.int32)
        query_pos = first + jnp.arange(TOK_DEV, dtype=jnp.int32)
        key_pos = first - BACK * TOK_DEV + jnp.arange(window, dtype=jnp.int32)
        doc_start = lax.optimization_barrier(jnp.max(jnp.where(starts[None, :] <= query_pos[:, None], starts[None, :], 0), axis=1))
        query_blk = lax.dynamic_slice_in_dim(query_feats, first, TOK_DEV, 0).reshape(TOK_DEV, H, HD).astype(jnp.float32)
        key_blk = lax.dynamic_slice_in_dim(key_pad, first, window, 0).reshape(window, KVH, HD).astype(jnp.float32)
        value_blk = lax.dynamic_slice_in_dim(value_pad, first, window, 0).reshape(window, KVH, HD).astype(jnp.float32)
        key_blk = jnp.repeat(key_blk, ratio, axis=1)
        value_blk = jnp.repeat(value_blk, ratio, axis=1)
        scores = jnp.einsum('qhd,khd->qhk', query_blk, key_blk, precision=lax.Precision.HIGHEST) * (1.0 / math.sqrt(HD))
        distance = query_pos[:, None] - key_pos[None, :]
        visible = (distance >= 0) & (key_pos[None, :] >= doc_start[:, None])
        weights = jnp.clip((span_end[None, :, None] - distance[:, None, :].astype(jnp.float32)) / ramp_float[None, :, None], 0.0, 1.0)
        weights = jnp.where(visible[:, None, :], weights, 0.0)
        limited = jnp.where(weights > 0.0, scores, very_low)
        top_score = lax.optimization_barrier(jnp.max(limited, axis=2))
        prob_terms = weights * jnp.exp(limited - top_score[:, :, None])
        denominator = lax.optimization_barrier(jnp.sum(prob_terms, axis=2))
        rounded = lax.optimization_barrier(prob_terms.astype(jnp.bfloat16)).astype(jnp.float32)
        numerator = jnp.einsum('qhk,khd->qhd', rounded, value_blk, precision=lax.Precision.HIGHEST)
        attended = (numerator / denominator[:, :, None]).astype(jnp.bfloat16).reshape(TOK_DEV, H * HD)
        mixed_sum = jnp.zeros((TOK_DEV, D), jnp.float32)
        for group in range(N_HEAD):
            low_col = group * group_width
            part_out = jnp.dot(attended[:, low_col:low_col + group_width], out_proj[:, low_col:low_col + group_width].T, preferred_element_type=jnp.float32)
            mixed_sum = mixed_sum + lax.optimization_barrier(part_out.astype(jnp.bfloat16)).astype(jnp.float32)
        return mixed_sum.astype(jnp.bfloat16)
    blocks = lax.map(one_block, jnp.arange(N_SEQ, dtype=jnp.int32))
    return blocks.reshape(N_SEQ * TOK_DEV, D)
```

```python
from functools import partial
import math

import jax
import jax.numpy as jnp
from jax import lax
from jax.experimental import pallas as pl
from jax.experimental.pallas import tpu as pltpu
from jax.sharding import PartitionSpec as P

HD = 128
TILE = 128
BACK = 4
LOW = -1e30
LOG2E = 1.4426950408889634


def attention_kernel(scal, reach_ref, q_hbm, s0, s1a, s1b, s2, s3a, s3b, s4, out_hbm,
                     q_v, k_v, v_v, out_v, acc_v, sem, out_sem):
    tok_rows, width = q_v.shape
    kv_width = k_v.shape[1]
    heads = width // HD
    ratio = heads // (kv_width // HD)
    q_tiles = tok_rows // TILE
    pad = TILE
    which = scal[0]

    q_copy = pltpu.make_async_copy(q_hbm, q_v, sem.at[0])
    q_copy.start()

    def copies(ref, slot):
        rows = pl.ds(pad + slot * tok_rows, tok_rows)
        return (
            pltpu.make_async_copy(ref.at[0], k_v.at[rows], sem.at[1 + slot]),
            pltpu.make_async_copy(ref.at[1], v_v.at[rows], sem.at[6 + slot]),
        )

    def begin(ref, slot):
        for copy in copies(ref, slot):
            copy.start()

    begin(s4, 4)

    @pl.when(which == 0)
    def _():
        begin(s3a, 3)
        begin(s1a, 1)

    @pl.when(which != 0)
    def _():
        begin(s3b, 3)
        begin(s1b, 1)

    begin(s2, 2)
    begin(s0, 0)
    k_v[0:pad, :] = jnp.zeros((pad, kv_width), k_v.dtype)
    v_v[0:pad, :] = jnp.zeros((pad, kv_width), v_v.dtype)
    q_copy.wait()
    for slot, ref in ((4, s4), (3, s3a), (2, s2), (1, s1a), (0, s0)):
        for copy in copies(ref, slot):
            copy.wait()

    min_reach = scal[1]
    max_reach = scal[2]
    scale = LOG2E / math.sqrt(HD)
    base = pad + BACK * tok_rows
    kk = lax.broadcasted_iota(jnp.int32, (2 * TILE, TILE), 0)
    qq = lax.broadcasted_iota(jnp.int32, (2 * TILE, TILE), 1)
    offset = (qq - kk).astype(jnp.float32)

    def one_head(head, carry):
        span = scal[3 + head]
        ramp = scal[3 + heads + head].astype(jnp.float32)
        inv_ramp = 1.0 / jnp.full((1, TILE), ramp, jnp.float32)
        q_cols = pl.ds(pl.multiple_of(head * HD, HD), HD)
        kv_cols = pl.ds(pl.multiple_of((head // ratio) * HD, HD), HD)
        last = jnp.minimum(span, (max_reach + TILE - 1) // TILE)
        steps = last // 2 + 1
        plain = jnp.minimum(steps, (min_reach + 1) // (2 * TILE))
        for t in range(q_tiles):
            acc_v[t] = jnp.zeros((HD, TILE), jnp.float32)

        def step(it, state, docs):
            shift = (2 * it + 1) * TILE
            shift_f = shift.astype(jnp.float32)
            left = (span * TILE).astype(jnp.float32) - shift_f - offset
            weight = jnp.minimum(left * inv_ramp, 1.0)
            seen = (left > 0.0) & (offset >= -shift_f)
            bias = jnp.where(seen, jnp.log2(jnp.where(seen, weight, 1.0)), LOW)
            tops, denoms = state
            new_tops, new_denoms = [], []
            for t in range(q_tiles):
                rows = pl.ds(pl.multiple_of(base + t * TILE - shift, TILE), 2 * TILE)
                keys = k_v[rows, kv_cols]
                queries = q_v[t * TILE:(t + 1) * TILE, q_cols]
                scores = lax.dot_general(
                    keys, queries, (((1,), (1,)), ((), ())), preferred_element_type=jnp.float32
                )
                tile_bias = bias
                if docs:
                    reach = reach_ref[0:1, t * TILE:(t + 1) * TILE] - shift_f
                    tile_bias = jnp.where(offset <= reach, bias, LOW)
                logits = scores * scale + tile_bias
                top = jnp.maximum(tops[t], jnp.max(logits, axis=0, keepdims=True))
                probs = jnp.exp2(logits - top)
                fade = jnp.exp2(tops[t] - top)
                new_tops.append(top)
                new_denoms.append(denoms[t] * fade + jnp.sum(probs, axis=0, keepdims=True))
                values = v_v[rows, kv_cols]
                update = lax.dot_general(
                    values, probs.astype(jnp.bfloat16), (((0,), (0,)), ((), ())),
                    preferred_element_type=jnp.float32,
                )
                acc_v[t] = acc_v[t] * fade + update
            return tuple(new_tops), tuple(new_denoms)

        state = (
            tuple(jnp.full((1, TILE), LOW, jnp.float32) for _ in range(q_tiles)),
            tuple(jnp.zeros((1, TILE), jnp.float32) for _ in range(q_tiles)),
        )
        state = lax.fori_loop(0, plain, partial(step, docs=False), state)
        state = lax.fori_loop(plain, steps, partial(step, docs=True), state)
        for t in range(q_tiles):
            result = acc_v[t] / state[1][t]
            out_v[t * TILE:(t + 1) * TILE, q_cols] = result.T.astype(out_v.dtype)
        return carry

    lax.fori_loop(0, heads, one_head, 0)
    out_copy = pltpu.make_async_copy(out_v, out_hbm, out_sem)
    out_copy.start()
    out_copy.wait()


def attention(scal, reach, queries, slots):
    tok_rows, width = queries.shape
    kv_width = slots[0].shape[2]
    rows = TILE + (BACK + 1) * tok_rows
    any_spec = pl.BlockSpec(memory_space=pl.ANY)
    return pl.pallas_call(
        attention_kernel,
        out_shape=jax.ShapeDtypeStruct((tok_rows, width), jnp.bfloat16),
        in_specs=[
            pl.BlockSpec(memory_space=pltpu.SMEM),
            pl.BlockSpec(memory_space=pltpu.VMEM),
        ] + [any_spec] * 8,
        out_specs=any_spec,
        scratch_shapes=[
            pltpu.VMEM((tok_rows, width), jnp.bfloat16),
            pltpu.VMEM((rows, kv_width), jnp.bfloat16),
            pltpu.VMEM((rows, kv_width), jnp.bfloat16),
            pltpu.VMEM((tok_rows, width), jnp.bfloat16),
            pltpu.VMEM((tok_rows // TILE, HD, TILE), jnp.float32),
            pltpu.SemaphoreType.DMA((11,)),
            pltpu.SemaphoreType.DMA,
        ],
        cost_estimate=pl.CostEstimate(
            flops=4 * tok_rows * width * 768, bytes_accessed=12 << 20, transcendentals=0
        ),
        name="span_attention",
    )(scal, reach, queries, *slots)


def project_kernel(count, place, att_hbm, *refs):
    w_hbm = refs[:count]
    keep_ref, send_ref = refs[count], refs[count + 1]
    att_v, w_v, sem = refs[count + 2:]
    half = keep_ref.shape[0]
    cols = w_v.shape[1]
    mine = place[0]
    att_copy = pltpu.make_async_copy(att_hbm, att_v, sem.at[count])
    att_copy.start()
    w_copies = [
        pltpu.make_async_copy(w_hbm[i], w_v.at[i], sem.at[i]) for i in range(count)
    ]
    for copy in w_copies:
        copy.start()
    att_copy.wait()
    for i in range(count):
        w_copies[i].wait()
        for ref, part in ((send_ref, 1 - mine), (keep_ref, mine)):
            rows = att_v[pl.ds(pl.multiple_of(part * half, half), half), :]
            ref[:, i * cols:(i + 1) * cols] = lax.dot_general(
                rows, w_v[i], (((1,), (1,)), ((), ())), preferred_element_type=jnp.float32
            ).astype(ref.dtype)


def project(place, attended, blocks):
    tok_rows, width = attended.shape
    cols = blocks[0].shape[0]
    count = len(blocks)
    half = jax.ShapeDtypeStruct((tok_rows // 2, count * cols), jnp.bfloat16)
    any_spec = pl.BlockSpec(memory_space=pl.ANY)
    return pl.pallas_call(
        partial(project_kernel, count),
        out_shape=(half, half),
        in_specs=[pl.BlockSpec(memory_space=pltpu.SMEM)] + [any_spec] * (count + 1),
        out_specs=(pl.BlockSpec(memory_space=pltpu.VMEM),) * 2,
        scratch_shapes=[
            pltpu.VMEM((tok_rows, width), jnp.bfloat16),
            pltpu.VMEM((count, cols, width), jnp.bfloat16),
            pltpu.SemaphoreType.DMA((count + 1,)),
        ],
        cost_estimate=pl.CostEstimate(
            flops=2 * tok_rows * width * cols * count,
            bytes_accessed=2 * width * (tok_rows + cols * count),
            transcendentals=0,
        ),
        name="project",
    )(place, attended, *blocks)


def finish_kernel(widths, cols_ref, *refs):
    n = len(widths)
    keeps, recvs = refs[:n], refs[n:2 * n]
    out_hbm, sum_v, sem = refs[2 * n:]
    copies = []
    place = 0
    for keep, recv, width in zip(keeps, recvs, widths):
        for low in range(0, keep.shape[1], width):
            sum_v[:, place:place + width] = (
                keep[:, low:low + width].astype(jnp.float32)
                + recv[:, low:low + width].astype(jnp.float32)
            ).astype(sum_v.dtype)
            i = len(copies)
            copy = pltpu.make_async_copy(
                sum_v.at[:, place:place + width],
                out_hbm.at[:, pl.ds(pl.multiple_of(cols_ref[i], HD), width)],
                sem.at[i],
            )
            copy.start()
            copies.append(copy)
            place += width
    for copy in copies:
        copy.wait()


def finish(columns, keeps, recvs, widths):
    rows = keeps[0].shape[0]
    total = sum(k.shape[1] for k in keeps)
    pieces = sum(k.shape[1] // w for k, w in zip(keeps, widths))
    vmem = pl.BlockSpec(memory_space=pltpu.VMEM)
    return pl.pallas_call(
        partial(finish_kernel, widths),
        out_shape=jax.ShapeDtypeStruct((rows, total), jnp.bfloat16),
        in_specs=[pl.BlockSpec(memory_space=pltpu.SMEM)] + [vmem] * (2 * len(keeps)),
        out_specs=pl.BlockSpec(memory_space=pl.ANY),
        scratch_shapes=[
            pltpu.VMEM((rows, total), jnp.bfloat16),
            pltpu.SemaphoreType.DMA((pieces,)),
        ],
        cost_estimate=pl.CostEstimate(flops=rows * total, bytes_accessed=6 * rows * total, transcendentals=0),
        name="finish",
    )(columns, *keeps, *recvs)


def after(value, *others):
    return lax.optimization_barrier((value,) + others)[0]


def scalars(span_class, ramp_width, doc_lengths, tok_rows, head_count, seq_index, head_index, which):
    query_pos = seq_index * tok_rows + jnp.arange(tok_rows, dtype=jnp.int32)
    starts = jnp.cumsum(doc_lengths) - doc_lengths
    doc_start = jnp.max(
        jnp.where(starts[None, :] <= query_pos[:, None], starts[None, :], 0), axis=1
    )
    reach = query_pos - doc_start
    local_span = lax.dynamic_slice_in_dim(span_class, head_index * head_count, head_count)
    local_ramp = lax.dynamic_slice_in_dim(ramp_width, head_index * head_count, head_count)
    head_part = jnp.stack([which, jnp.min(reach), jnp.max(reach)]).astype(jnp.int32)
    scal = jnp.concatenate([head_part, local_span, local_ramp])
    return scal, jnp.broadcast_to(reach.astype(jnp.float32)[None, :], (8, tok_rows))


def plain_device(query_feats, key_feats, value_feats, span_class, ramp_width, doc_lengths, out_proj):
    tok_rows, feat_width = query_feats.shape
    n_seq = lax.axis_size("seq")
    seq_index = lax.axis_index("seq")
    scal, reach = scalars(
        span_class, ramp_width, doc_lengths, tok_rows, feat_width // HD,
        seq_index, lax.axis_index("head"), jnp.int32(0),
    )
    own = jnp.stack([key_feats, value_feats])
    back = [
        lax.ppermute(own, "seq", [(i - d, i) for i in range(d, n_seq)])
        for d in range(1, BACK + 1)
    ]
    slots = (back[3], back[2], back[2], back[1], back[0], back[0], own)
    attended = attention(scal, reach, query_feats, slots)
    partials = lax.dot_general(
        attended,
        lax.all_gather(out_proj, "seq", axis=0, tiled=True),
        (((1,), (1,)), ((), ())),
        preferred_element_type=jnp.float32,
    )
    return lax.psum_scatter(partials.astype(jnp.bfloat16), "head", scatter_dimension=0, tiled=True)


def split_device(query_feats, key_feats, value_feats, span_class, ramp_width, doc_lengths, out_proj):
    tok_rows, feat_width = query_feats.shape
    zs, ys, cs = lax.axis_size("seq") // 4, 2, 2
    seq_index = lax.axis_index("seq")
    head_index = lax.axis_index("head")
    z, y, c = seq_index // 4, (seq_index // 2) % 2, seq_index % 2
    place = [(a, b, d) for a in range(zs) for b in range(ys) for d in range(cs)]

    def send(block, rule):
        pairs = []
        for src, (a, b, d) in enumerate(place):
            target = rule(a, b, d)
            if target is not None and 0 <= target[0] < zs:
                pairs.append((src, target[0] * 4 + target[1] * 2 + target[2]))
        return lax.ppermute(block, "seq", pairs)

    def core_swap(block):
        return send(block, lambda a, b, d: (a, b, 1 - d))

    def y_swap(block):
        return send(block, lambda a, b, d: (a, 1 - b, d))

    def z_turn(block, k):
        return send(block, lambda a, b, d: ((a + zs - k) % zs, b, d))

    scal, reach = scalars(
        span_class, ramp_width, doc_lengths, tok_rows, feat_width // HD, seq_index, head_index, c
    )
    own = jnp.stack([key_feats, value_feats])
    below = send(own, lambda a, b, d: (a + 1, b, d))
    beside = send(own, lambda a, b, d: (a, 1, d) if b == 0 else None)
    w_y = [y_swap(out_proj)]
    own_sw = core_swap(own)
    relay = send(below, lambda a, b, d: (a, 0, d) if b == 1 else None)
    w_z = [out_proj]
    w_z.append(z_turn(after(out_proj, below), 3))
    below_sw = core_swap(below)
    prev = jnp.where(y == 1, beside, relay)
    prev_sw = core_swap(prev)
    w_z.append(z_turn(after(out_proj, w_z[1]), 1))
    half = out_proj.shape[0] // 2
    w_z.append(z_turn(after(out_proj[:half], w_z[2]), 2))
    w_z.append(z_turn(after(out_proj[half:], w_z[2]), 2))
    w_y += [y_swap(block) for block in w_z[1:]]

    attended = attention(
        scal, reach, query_feats, (below, below_sw, prev_sw, prev, prev_sw, own_sw, own)
    )

    where_x = jnp.reshape(head_index, (1,)).astype(jnp.int32)
    keeps, recvs, widths, columns = [], [], [], []
    rows_w = out_proj.shape[0]
    for k, low, near, far in zip((0, 3, 1, 2, 2), (0, 0, 0, 0, half), w_z, w_y):
        near_sw, far_sw = core_swap(near), core_swap(far)
        keep, away = project(where_x, attended, (near, near_sw, far, far_sw))
        recv = lax.ppermute(away, "head", [(0, 1), (1, 0)])
        keeps.append(keep)
        recvs.append(recv)
        widths.append(near.shape[0])
        zz = (z + k) % zs
        for yy, cc in ((y, c), (y, 1 - c), (1 - y, c), (1 - y, 1 - c)):
            columns.append((zz * 4 + yy * 2 + cc) * rows_w + low)
    return finish(jnp.stack(columns).astype(jnp.int32), keeps, recvs, widths)


def solution(mesh):
    in_specs = (
        P("seq", "head"),
        P("seq", "head"),
        P("seq", "head"),
        P(),
        P(),
        P(),
        P("seq", "head"),
    )
    out_specs = P(("seq", "head"), None)
    special = mesh.shape["seq"] == 16 and mesh.shape["head"] == 2
    return jax.shard_map(
        split_device if special else plain_device,
        mesh=mesh, in_specs=in_specs, out_specs=out_specs, check_vma=False,
    )
```
